1024 devices in a mesh: blk: 128 (over y, z_lo, core), ulysses: 8 (over z_hi, x).
Axes of the slice: x: 4, y: 4, z: 32 (z_hi: 2, z_lo: 16; z = z_hi * 16 + z_lo), core: 2. Of those that a mesh axis runs over, the one named last changes fastest.
Arguments:
- queries: bfloat16 [131072, 2048], P(('blk', 'ulysses')), may hold values from -6 to 6
- key_states: bfloat16 [131072, 512], P(('blk', 'ulysses')), may hold values from -6 to 6
- value_states: bfloat16 [131072, 512], P(('blk', 'ulysses')), may hold values from -6 to 6
- attn_out: bfloat16 [131072, 2048], P(('blk', 'ulysses')), may hold values from -6 to 6
- grad_out: bfloat16 [131072, 2048], P(('blk', 'ulysses')), may hold values from -6 to 6
- log_sums: float32 [131072, 32], P(('blk', 'ulysses')), may hold values from 2 to 4
- owners: int32 [256], replicated, may hold values from 0 to 255, as said below
Outputs:
- grad_query: bfloat16 [131072, 2048], P(('blk', 'ulysses'))
- grad_key: bfloat16 [131072, 512], P(('blk', 'ulysses'))
- grad_value: bfloat16 [131072, 512], P(('blk', 'ulysses'))
The draws below stay inside these ranges and needn't reach their ends.
Inputs may be any that keep to these rules, and one draw needn't show every extreme that they name: `owners`: every value 0 to 255 appears exactly once; each sequence block holds one half-block below 128 and the half-block 2 * 128 - 1 minus it.
All inputs are finite; a program needn't handle non-finite values.
Results may differ from the reference program's by a relative error of at most 0.0049.
Values may be sent and summed in bfloat16 or wider, within the bound.
A program may use at most 32 MiB of HBM per device.

```python
import math
import jax
import jax.numpy as jnp
from jax import lax

HEADS = 32
KV_HEADS = 8
HEAD_DIM = 64
TOK_DEV = 128
SEQ = 131072
N_BLK = 128
N_ULYSSES = 8


def draw_owners(key, part):
    first_key = jax.random.fold_in(key, 11)
    second_key = jax.random.fold_in(key, 23)
    lower = jax.random.permutation(first_key, N_BLK).astype(jnp.int32)
    flipped = jax.random.randint(second_key, (N_BLK,), 0, 2).astype(jnp.int32)
    upper = (2 * N_BLK - 1 - lower).astype(jnp.int32)
    leading = jnp.where(flipped == 1, upper, lower)
    trailing = jnp.where(flipped == 1, lower, upper)
    return jnp.stack([leading, trailing], axis=1).reshape(-1).astype(jnp.int32)


def steps_of(key, dims, split, least, high):
    loudness, own = 1.0, jax.random.fold_in(key, 6)
    for axis_at, blocks in split:
        draws = jnp.exp(jax.random.uniform(jax.random.fold_in(own, axis_at), (blocks,), jnp.float32, least / len(split), high / len(split)))
        loudness = loudness * jnp.repeat(draws, dims[axis_at] // blocks).reshape([-1 if axis == axis_at else 1 for axis in range(len(dims))])
    return loudness


def bell_draw(rng, dims, spread, most, pieces=(), kind=jnp.bfloat16):
    entries = spread * jax.random.normal(rng, dims, jnp.float32)
    if pieces:
        entries = entries * steps_of(rng, dims, pieces, -0.22, 0.18)
    return jnp.clip(entries, -most, most).astype(kind)


def setup_inputs(seed: int = 0) -> dict:
    keys = jax.random.split(jax.random.key(seed), 8)
    return {
        "queries": bell_draw(keys[0], (SEQ, HEADS * HEAD_DIM), 1.0, 6.0, ((0, 1024),)),
        "key_states": bell_draw(keys[1], (SEQ, KV_HEADS * HEAD_DIM), 1.0, 6.0, ((0, 1024),)),
        "value_states": bell_draw(keys[2], (SEQ, KV_HEADS * HEAD_DIM), 1.0, 6.0, ((0, 1024),)),
        "attn_out": bell_draw(keys[3], (SEQ, HEADS * HEAD_DIM), 1.0, 6.0, ((0, 1024),)),
        "grad_out": bell_draw(keys[4], (SEQ, HEADS * HEAD_DIM), 1.0, 6.0, ((0, 1024),)),
        "log_sums": jnp.clip(2.0 + 2.0 * jax.random.uniform(keys[5], (SEQ, HEADS), jnp.float32) ** steps_of(keys[5], (SEQ, HEADS), ((0, 1024),), -0.2, 0.2), 2.0, 4.0),
        "owners": draw_owners(jax.random.fold_in(keys[7], 71), 0),
    }


def block_grads(query_blk, grad_blk, key_blk, value_blk, sums_blk, delta_blk, query_pos, key_pos):
    wide = jnp.float32
    factor = 1.0 / math.sqrt(HEAD_DIM)
    scores = jnp.einsum('qhgd,khd->hgqk', query_blk.astype(wide), key_blk.astype(wide)) * factor
    sums_t = jnp.transpose(sums_blk, (1, 2, 0))[..., None]
    delta_t = jnp.transpose(delta_blk, (1, 2, 0))[..., None]
    visible = query_pos[:, None] >= key_pos[None, :]
    probs = jnp.where(visible, jnp.exp(scores - sums_t), 0.0)
    probs_b = probs.astype(jnp.bfloat16)
    grad_value = jnp.einsum('hgqk,qhgd->khd', probs_b.astype(wide), grad_blk.astype(wide))
    dprobs = jnp.einsum('qhgd,khd->hgqk', grad_blk.astype(wide), value_blk.astype(wide))
    dscores = (probs * (dprobs - delta_t) * factor).astype(jnp.bfloat16)
    grad_query = jnp.einsum('hgqk,khd->qhgd', dscores.astype(wide), key_blk.astype(wide))
    grad_key = jnp.einsum('hgqk,qhgd->khd', dscores.astype(wide), query_blk.astype(wide))
    count = query_blk.shape[0]
    return (grad_query.astype(jnp.bfloat16).reshape(count, -1), grad_key.astype(jnp.bfloat16).reshape(count, -1), grad_value.astype(jnp.bfloat16).reshape(count, -1))

def select_rank(array, index):
    return lax.dynamic_index_in_dim(array, index, 0, keepdims=False)

def reference(queries, key_states, value_states, attn_out, grad_out, log_sums, owners):
    group_tok = TOK_DEV * N_ULYSSES
    half = group_tok // 2
    group = HEADS // KV_HEADS
    delta = lax.optimization_barrier(jnp.sum((grad_out.astype(jnp.float32) * attn_out.astype(jnp.float32)).reshape(-1, HEADS, HEAD_DIM), axis=2))
    query_shape = (N_BLK, group_tok, KV_HEADS, group, HEAD_DIM)
    query_all = queries.reshape(query_shape)
    grad_all = grad_out.reshape(query_shape)
    key_all = key_states.reshape(N_BLK, group_tok, KV_HEADS, HEAD_DIM)
    value_all = value_states.reshape(N_BLK, group_tok, KV_HEADS, HEAD_DIM)
    sums_all = log_sums.reshape(N_BLK, group_tok, KV_HEADS, group)
    delta_all = delta.reshape(N_BLK, group_tok, KV_HEADS, group)
    offsets = jnp.arange(group_tok, dtype=jnp.int32)

    def one_rank(rank):
        before = (rank - 1) % N_BLK
        query_pos = jnp.take(owners, 2 * rank + offsets // half) * half + offsets % half
        key_pos = jnp.take(owners, 2 * before + offsets // half) * half + offsets % half
        return block_grads(select_rank(query_all, rank), select_rank(grad_all, rank), select_rank(key_all, before), select_rank(value_all, before), select_rank(sums_all, rank), select_rank(delta_all, rank), query_pos, key_pos)
    grad_query, grad_key, grad_value = lax.map(one_rank, jnp.arange(N_BLK, dtype=jnp.int32))
    grad_query = grad_query.reshape(-1, HEADS * HEAD_DIM)
    grad_key = jnp.roll(grad_key, -1, axis=0).reshape(-1, KV_HEADS * HEAD_DIM)
    grad_value = jnp.roll(grad_value, -1, axis=0).reshape(-1, KV_HEADS * HEAD_DIM)
    return (grad_query, grad_key, grad_value)
```

```python
import functools
import math

import jax
import jax.numpy as jnp
from jax import lax
from jax.experimental import pallas as pl
from jax.experimental.pallas import tpu as pltpu
from jax.sharding import PartitionSpec as P

HEAD_DIM = 64
LANES = 128
TOK = 128
RING = 4
HALF = TOK * RING
HEADS_LOCAL = 8
PAIRS = HEADS_LOCAL // 2
WIDTH = HEADS_LOCAL * HEAD_DIM
CROSS = 8
CROSS_ROWS = HALF // CROSS
AHEAD = 4
SLOTS = CROSS + AHEAD
LOCAL = 4
LOCAL_ROWS = HALF // LOCAL
PER_DEVICE = TOK // CROSS_ROWS
HIDE = 1e30
MESH = pl.DeviceIdType.MESH


def dot_nt(a, b):
    return lax.dot_general(a, b, (((1,), (1,)), ((), ())), preferred_element_type=jnp.float32)


def dot(a, b):
    return jnp.dot(a, b, preferred_element_type=jnp.float32)


def chunk_grads(key, value, sums_ref, delta_ref, query_ref, grad_ref, acc_ref):
    rows = key.shape[0]
    low = lax.broadcasted_iota(jnp.int32, (rows, LANES), 1) < HEAD_DIM
    zero = jnp.zeros((rows, LANES), jnp.float32)

    def spread(array, head):
        rolled = pltpu.roll(array, HEAD_DIM, 1)
        first, second = (array, rolled) if head == 0 else (rolled, array)
        return jnp.concatenate([jnp.where(low, first, zero), jnp.where(low, zero, second)], axis=0)

    def gather(first, second):
        one = first[:rows] + pltpu.roll(first[rows:], HEAD_DIM, 1)
        two = pltpu.roll(second[:rows], HEAD_DIM, 1) + second[rows:]
        return jnp.where(low, one, two)

    factor = 1.0 / math.sqrt(HEAD_DIM)
    key_f = key.astype(jnp.float32)
    value_f = value.astype(jnp.float32) * factor
    key_sums, value_sums = [], []
    for head in range(2):
        key_wide = spread(key_f, head)
        key_turned = key_wide.T.astype(jnp.bfloat16)
        key_wide = (key_wide * factor).astype(jnp.bfloat16)
        value_wide = spread(value_f, head).astype(jnp.bfloat16)
        key_sum, value_sum = None, None
        for pair in (2 * head, 2 * head + 1):
            cols = pl.ds(pair * LANES, LANES)
            query, grad = query_ref[:, cols], grad_ref[:, cols]
            scores = dot_nt(key_wide, query)
            dprobs = dot_nt(value_wide, grad)
            probs_b, dscores = [], []
            for one in range(2):
                part = slice(one * rows, (one + 1) * rows)
                at = pl.ds(2 * pair + one, 1)
                probs = jnp.exp(scores[part] - sums_ref[at, :])
                probs_b.append(probs.astype(jnp.bfloat16))
                dscores.append((probs * (dprobs[part] - delta_ref[at, :])).astype(jnp.bfloat16))
            probs_b = jnp.concatenate(probs_b, axis=0)
            dscores = jnp.concatenate(dscores, axis=0)
            value_piece, key_piece = dot(probs_b, grad), dot(dscores, query)
            value_sum = value_piece if value_sum is None else value_sum + value_piece
            key_sum = key_piece if key_sum is None else key_sum + key_piece
            acc_ref[cols, :] += dot(key_turned, dscores)
        key_sums.append(key_sum)
        value_sums.append(value_sum)
    return (gather(*key_sums), gather(*value_sums))


def kernel(
    n_blk,
    query_in,
    grad_in,
    key_in,
    value_in,
    stats_in,
    marks,
    query_out,
    both_out,
    query_g,
    grad_g,
    both_g,
    stats_g,
    sums_hid,
    acc,
    kept,
    slots,
    staged,
    query_s,
    both_s,
    wide_send,
    wide_recv,
    both_send,
    both_recv,
    slot_send,
    slot_recv,
    back_send,
    back_recv,
    out_send,
    out_recv,
    own_sem,
):
    blk, lane = lax.axis_index("blk"), lax.axis_index("ulysses")
    x, side = lax.rem(lane, RING), lane // RING
    after, before = lax.rem(blk + 1, n_blk), lax.rem(blk + n_blk - 1, n_blk)
    across = (blk, (1 - side) * RING + x)

    def peer(step):
        return lax.rem(x + step, RING)

    def at_x(block, where):
        return (block, side * RING + where)

    def remote(src, dst, send, recv, device):
        return pltpu.make_async_remote_copy(
            src_ref=src, dst_ref=dst, send_sem=send, recv_sem=recv, device_id=device, device_id_type=MESH
        )

    barrier = pltpu.get_barrier_semaphore()
    friends = [across] + [at_x(blk, peer(step)) for step in range(1, RING)]
    friends += [at_x(block, peer(step)) for block in (after, before) for step in range(RING)]
    for friend in friends:
        pl.semaphore_signal(barrier, inc=1, device_id=friend, device_id_type=MESH)
    acc[...] = jnp.zeros_like(acc)
    pl.semaphore_wait(barrier, len(friends))

    def rows_of(where):
        return pl.ds(pl.multiple_of(where * TOK, TOK), TOK)

    mine = rows_of(x)

    def both_copy(step, which):
        to = peer(step)
        cols = pl.ds(pl.multiple_of(to * LANES, LANES), LANES)
        src = (key_in, value_in)[which].at[:, cols]
        return remote(
            src, both_g.at[which, mine], both_send.at[step, which], both_recv.at[step, which], at_x(after, to)
        )

    for step in range(RING):
        for which in range(2):
            both_copy(step, which).start()

    def wide_parts(to):
        cols = pl.ds(pl.multiple_of(to * WIDTH, LANES), WIDTH)
        heads = pl.ds(pl.multiple_of(to * HEADS_LOCAL, HEADS_LOCAL), HEADS_LOCAL)
        lanes = pl.ds(pl.multiple_of(x * TOK, LANES), TOK)
        return (
            (query_in.at[:, cols], query_g.at[mine]),
            (grad_in.at[:, cols], grad_g.at[mine]),
            (stats_in.at[:, heads], stats_g.at[:, :, lanes]),
        )

    def wide_copy(step, which):
        src, dst = wide_parts(peer(step))[which]
        return remote(
            src, dst, wide_send.at[step - 1, which], wide_recv.at[step - 1, which], at_x(blk, peer(step))
        )

    for which in (2, 0, 1):
        for step in range(1, RING):
            wide_copy(step, which).start()
    own = [pltpu.make_async_copy(src, dst, own_sem.at[i]) for i, (src, dst) in enumerate(wide_parts(x))]
    for copy in own:
        copy.start()

    for step in range(RING):
        for which in range(2):
            both_copy(step, which).wait_recv()

    def chunk_rows(t, rows):
        return pl.ds(pl.multiple_of(t * rows, rows), rows)

    def first_copy(t):
        src = both_g.at[:, chunk_rows(t, CROSS_ROWS)]
        return remote(src, slots.at[t], slot_send.at[t], slot_recv.at[t], across)

    def later_copy(t):
        return remote(staged.at[t], slots.at[t + AHEAD], slot_send.at[t + AHEAD], slot_recv.at[t + AHEAD], across)

    for t in range(AHEAD):
        first_copy(t).start()

    for copy in own:
        copy.wait()
    for which in (2, 0, 1):
        for step in range(1, RING):
            wide_copy(step, which).wait_recv()

    for i in range(2):
        sums_hid[i] = stats_g[0] + jnp.concatenate([marks[i]] * RING, axis=1)

    grads = functools.partial(
        chunk_grads, delta_ref=stats_g.at[1], query_ref=query_g, grad_ref=grad_g, acc_ref=acc
    )

    def local_step(t, carry):
        rows = chunk_rows(t, LOCAL_ROWS)
        kept[0, rows], kept[1, rows] = grads(both_g[0, rows], both_g[1, rows], sums_hid.at[0])
        return carry

    lax.fori_loop(0, LOCAL, local_step, 0)

    gives = jnp.broadcast_to(marks[2, 0:1, :], (CROSS_ROWS, LANES)) > 0.5

    def slot_copy(t):
        return remote(slots.at[t], slots.at[t], slot_send.at[t], slot_recv.at[t], across)

    def out_copy(t):
        part = lax.rem(t, PER_DEVICE)
        rows = chunk_rows(part, CROSS_ROWS)
        cols = pl.ds(pl.multiple_of(x * LANES, LANES), LANES)
        return remote(
            both_s.at[t],
            both_out.at[:, rows, cols],
            out_send.at[t],
            out_recv.at[x, part],
            at_x(before, t // PER_DEVICE),
        )

    def finish(t):
        rows = chunk_rows(t, CROSS_ROWS)
        for which in range(2):
            came = jnp.where(gives, slots[t + AHEAD, which].astype(jnp.float32), 0.0)
            both_s[t, which] = (kept[which, rows] + came).astype(jnp.bfloat16)
        out_copy(t).start()

    def cross_step(t, carry):
        slot_copy(t).wait_recv()
        far = [jnp.where(gives, 0.0, slots[t, which].astype(jnp.float32)) for which in range(2)]
        out = grads(far[0], far[1], sums_hid.at[1])
        rows = chunk_rows(jnp.minimum(t + AHEAD, CROSS - 1), CROSS_ROWS)
        for which in range(2):
            given = both_g[which, rows].astype(jnp.float32)
            staged[t, which] = jnp.where(gives, given, out[which]).astype(jnp.bfloat16)
        later_copy(t).start()

        @pl.when(t >= AHEAD)
        def _():
            finish(t - AHEAD)

        return carry

    lax.fori_loop(0, CROSS, cross_step, 0)

    def back_copy(step):
        cols = pl.ds(pl.multiple_of(x * WIDTH, LANES), WIDTH)
        return remote(
            query_s.at[step],
            query_out.at[:, cols],
            back_send.at[step - 1],
            back_recv.at[step - 1],
            at_x(blk, peer(step)),
        )

    for step in (1, 2, 3, 0):
        lanes = pl.ds(pl.multiple_of(peer(step) * TOK, LANES), TOK)
        turned = acc[:, lanes].T.astype(jnp.bfloat16)
        if step == 0:
            query_out[:, pl.ds(pl.multiple_of(x * WIDTH, LANES), WIDTH)] = turned
        else:
            query_s[step] = turned
            back_copy(step).start()

    def last_step(t, carry):
        slot_copy(t).wait_recv()
        finish(t - AHEAD)
        return carry

    lax.fori_loop(CROSS, SLOTS, last_step, 0)

    for step in range(1, RING):
        back_copy(step).wait_recv()

    def arrived(i, carry):
        where, part = i // PER_DEVICE, lax.rem(i, PER_DEVICE)
        cols = pl.ds(pl.multiple_of(where * LANES, LANES), LANES)
        dst = both_out.at[:, chunk_rows(part, CROSS_ROWS), cols]
        remote(both_s.at[0], dst, out_send.at[0], out_recv.at[where, part], across).wait_recv()
        return carry

    lax.fori_loop(0, RING * PER_DEVICE, arrived, 0)

    for step in range(RING):
        for which in range(2):
            both_copy(step, which).wait_send()
    for step in range(1, RING):
        for which in range(3):
            wide_copy(step, which).wait_send()
        back_copy(step).wait_send()
    for t in range(AHEAD):
        first_copy(t).wait_send()
    for t in range(CROSS):
        later_copy(t).wait_send()
        out_copy(t).wait_send()


def per_device(n_blk, queries, key_states, value_states, attn_out, grad_out, log_sums, owners):
    heads = log_sums.shape[1]
    wide = jnp.float32
    delta = jnp.sum((grad_out.astype(wide) * attn_out.astype(wide)).reshape(TOK, heads, HEAD_DIM), axis=2)
    stats = jnp.stack([log_sums.T, delta.T * (1.0 / math.sqrt(HEAD_DIM))])
    blk, side = lax.axis_index("blk"), lax.axis_index("ulysses") // RING
    before = (blk + n_blk - 1) % n_blk
    query_half = owners[2 * blk + side]
    sees_near = query_half > owners[2 * before + side]
    sees_far = query_half > owners[2 * before + 1 - side]
    marks = jnp.stack(
        [jnp.where(sees_near, 0.0, HIDE), jnp.where(sees_far, 0.0, HIDE), jnp.where(sees_far, 0.0, 1.0)]
    ).astype(wide)
    marks = jnp.broadcast_to(marks[:, None, None], (3, HEADS_LOCAL, LANES))
    hbm, vmem = pl.BlockSpec(memory_space=pl.ANY), pl.BlockSpec(memory_space=pltpu.VMEM)
    narrow = jnp.bfloat16
    dma = pltpu.SemaphoreType.DMA
    grad_query, both = pl.pallas_call(
        functools.partial(kernel, n_blk),
        out_shape=(
            jax.ShapeDtypeStruct((TOK, heads * HEAD_DIM), narrow),
            jax.ShapeDtypeStruct((2, TOK, RING * LANES), narrow),
        ),
        in_specs=[hbm, hbm, hbm, hbm, vmem, vmem],
        out_specs=(vmem, vmem),
        scratch_shapes=[
            pltpu.VMEM((HALF, WIDTH), narrow),
            pltpu.VMEM((HALF, WIDTH), narrow),
            pltpu.VMEM((2, HALF, LANES), narrow),
            pltpu.VMEM((2, HEADS_LOCAL, HALF), wide),
            pltpu.VMEM((2, HEADS_LOCAL, HALF), wide),
            pltpu.VMEM((WIDTH, HALF), wide),
            pltpu.VMEM((2, HALF, LANES), wide),
            pltpu.VMEM((SLOTS, 2, CROSS_ROWS, LANES), narrow),
            pltpu.VMEM((CROSS, 2, CROSS_ROWS, LANES), narrow),
            pltpu.VMEM((RING, TOK, WIDTH), narrow),
            pltpu.VMEM((CROSS, 2, CROSS_ROWS, LANES), narrow),
            dma((RING - 1, 3)),
            dma((RING - 1, 3)),
            dma((RING, 2)),
            dma((RING, 2)),
            dma((SLOTS,)),
            dma((SLOTS,)),
            dma((RING - 1,)),
            dma((RING - 1,)),
            dma((CROSS,)),
            dma((RING, PER_DEVICE)),
            dma((3,)),
        ],
        compiler_params=pltpu.CompilerParams(
            collective_id=0, has_side_effects=True, vmem_limit_bytes=48 * 1024 * 1024
        ),
    )(queries, grad_out, key_states, value_states, stats, marks)
    return (grad_query, both[0], both[1])


def solution(mesh):
    rows = P(("blk", "ulysses"), None)
    return jax.shard_map(
        functools.partial(per_device, mesh.shape["blk"]),
        mesh=mesh,
        in_specs=(rows, rows, rows, rows, rows, rows, P(None)),
        out_specs=(rows, rows, rows),
        check_vma=False,
    )
```

```python
import functools
import math

import jax
import jax.numpy as jnp
from jax import lax
from jax.experimental import pallas as pl
from jax.experimental.pallas import tpu as pltpu
from jax.sharding import PartitionSpec as P

HEAD_DIM = 64
LANES = 128
TOK = 128
RING = 4
HALF = TOK * RING
HEADS_LOCAL = 8
PAIRS = HEADS_LOCAL // 2
WIDTH = HEADS_LOCAL * HEAD_DIM
CROSS = 16
CROSS_ROWS = HALF // CROSS
AHEAD = 5
SLOTS = CROSS + AHEAD
PER_DEVICE = TOK // CROSS_ROWS
TURN = 32
HIDE = 1e30
MESH = pl.DeviceIdType.MESH


def dot_nt(a, b):
    return lax.dot_general(a, b, (((1,), (1,)), ((), ())), preferred_element_type=jnp.float32)


def dot(a, b):
    return jnp.dot(a, b, preferred_element_type=jnp.float32)


def chunk_grads(key, value, sums_ref, delta_ref, query_ref, grad_ref, acc_ref):
    rows = key.shape[0]
    low = lax.broadcasted_iota(jnp.int32, (rows, LANES), 1) < HEAD_DIM
    zero = jnp.zeros((rows, LANES), jnp.float32)

    def spread(array, head):
        rolled = pltpu.roll(array, HEAD_DIM, 1)
        first, second = (array, rolled) if head == 0 else (rolled, array)
        return jnp.concatenate([jnp.where(low, first, zero), jnp.where(low, zero, second)], axis=0)

    def gather(first, second):
        one = first[:rows] + pltpu.roll(first[rows:], HEAD_DIM, 1)
        two = pltpu.roll(second[:rows], HEAD_DIM, 1) + second[rows:]
        return jnp.where(low, one, two)

    factor = 1.0 / math.sqrt(HEAD_DIM)
    key_f = key.astype(jnp.float32)
    value_f = value.astype(jnp.float32) * factor
    key_sums, value_sums = [], []
    for head in range(2):
        key_wide = spread(key_f, head)
        key_turned = key_wide.T.astype(jnp.bfloat16)
        key_wide = (key_wide * factor).astype(jnp.bfloat16)
        value_wide = spread(value_f, head).astype(jnp.bfloat16)
        key_sum, value_sum = None, None
        for pair in (2 * head, 2 * head + 1):
            cols = pl.ds(pair * LANES, LANES)
            query, grad = query_ref[:, cols], grad_ref[:, cols]
            scores = dot_nt(key_wide, query)
            dprobs = dot_nt(value_wide, grad)
            probs_b, dscores = [], []
            for one in range(2):
                part = slice(one * rows, (one + 1) * rows)
                at = pl.ds(2 * pair + one, 1)
                probs = jnp.exp(scores[part] - sums_ref[at, :])
                probs_b.append(probs.astype(jnp.bfloat16))
                dscores.append((probs * (dprobs[part] - delta_ref[at, :])).astype(jnp.bfloat16))
            probs_b = jnp.concatenate(probs_b, axis=0)
            dscores = jnp.concatenate(dscores, axis=0)
            value_piece, key_piece = dot(probs_b, grad), dot(dscores, query)
            value_sum = value_piece if value_sum is None else value_sum + value_piece
            key_sum = key_piece if key_sum is None else key_sum + key_piece
            acc_ref[cols, :] += dot(key_turned, dscores)
        key_sums.append(key_sum)
        value_sums.append(value_sum)
    return (gather(*key_sums), gather(*value_sums))


def kernel(
    n_blk,
    query_in,
    grad_in,
    key_in,
    value_in,
    out_in,
    sums_in,
    owners,
    query_out,
    both_out,
    grad_v,
    out_v,
    stats_in,
    query_g,
    grad_g,
    both_g,
    stats_g,
    sums_hid,
    acc,
    kept,
    slots,
    staged,
    query_s,
    both_s,
    wide_send,
    wide_recv,
    both_send,
    both_recv,
    slot_send,
    slot_recv,
    back_send,
    back_recv,
    out_send,
    out_recv,
    own_sem,
    load_sem,
):
    blk, lane = lax.axis_index("blk"), lax.axis_index("ulysses")
    x, side = lax.rem(lane, RING), lane // RING
    after, before = lax.rem(blk + 1, n_blk), lax.rem(blk + n_blk - 1, n_blk)
    across = (blk, (1 - side) * RING + x)

    def turned(block):
        wraps = jnp.where(lax.rem(block, TURN) == 0, 1, 0)
        return lax.rem(side + wraps, 2)

    near = {"after": (after, turned(after)), "before": (before, turned(blk)), "same": (blk, side)}

    def peer(step):
        return lax.rem(x + step, RING)

    def at_x(name, where):
        block, half = near[name]
        return (block, half * RING + where)

    def remote(src, dst, send, recv, device):
        return pltpu.make_async_remote_copy(
            src_ref=src, dst_ref=dst, send_sem=send, recv_sem=recv, device_id=device, device_id_type=MESH
        )

    barrier = pltpu.get_barrier_semaphore()
    friends = [across] + [at_x("same", peer(step)) for step in range(1, RING)]
    friends += [at_x(name, peer(step)) for name in ("after", "before") for step in range(RING)]
    for friend in friends:
        pl.semaphore_signal(barrier, inc=1, device_id=friend, device_id_type=MESH)

    loads = [
        pltpu.make_async_copy(src, dst, load_sem.at[i])
        for i, (src, dst) in enumerate(((grad_in, grad_v), (out_in, out_v), (sums_in, stats_in.at[0])))
    ]
    for copy in loads:
        copy.start()
    acc[...] = jnp.zeros_like(acc)
    query_half = jnp.full((HEADS_LOCAL, LANES), owners[2 * blk + side], jnp.int32)
    near_half = jnp.full((HEADS_LOCAL, LANES), owners[2 * before + near["before"][1]], jnp.int32)
    far_half = jnp.full((HEADS_LOCAL, LANES), owners[2 * before + 1 - near["before"][1]], jnp.int32)
    marks = [jnp.where(query_half > other, 0.0, HIDE) for other in (near_half, far_half)]
    for copy in loads:
        copy.wait()
    factor = 1.0 / math.sqrt(HEAD_DIM)
    for i in range(grad_v.shape[1] // LANES):
        cols = pl.ds(i * LANES, LANES)
        product = (grad_v[:, cols].astype(jnp.float32) * out_v[:, cols].astype(jnp.float32)).T
        for one in range(2):
            total = jnp.sum(product[one * HEAD_DIM : (one + 1) * HEAD_DIM], axis=0, keepdims=True)
            stats_in[1, pl.ds(2 * i + one, 1), :] = total * factor

    pl.semaphore_wait(barrier, len(friends))

    def rows_of(where):
        return pl.ds(pl.multiple_of(where * TOK, TOK), TOK)

    mine = rows_of(x)

    def both_copy(step, which):
        to = peer(step)
        cols = pl.ds(pl.multiple_of(to * LANES, LANES), LANES)
        src = (key_in, value_in)[which].at[:, cols]
        return remote(
            src, both_g.at[which, mine], both_send.at[step, which], both_recv.at[step, which], at_x("after", to)
        )

    for step in range(RING):
        for which in range(2):
            both_copy(step, which).start()

    def wide_parts(to):
        cols = pl.ds(pl.multiple_of(to * WIDTH, LANES), WIDTH)
        heads = pl.ds(pl.multiple_of(to * HEADS_LOCAL, HEADS_LOCAL), HEADS_LOCAL)
        lanes = pl.ds(pl.multiple_of(x * TOK, LANES), TOK)
        return (
            (query_in.at[:, cols], query_g.at[mine]),
            (grad_in.at[:, cols], grad_g.at[mine]),
            (stats_in.at[:, heads], stats_g.at[:, :, lanes]),
        )

    def wide_copy(step, which):
        src, dst = wide_parts(peer(step))[which]
        return remote(
            src, dst, wide_send.at[step - 1, which], wide_recv.at[step - 1, which], at_x("same", peer(step))
        )

    for which in (2, 0, 1):
        for step in range(1, RING):
            wide_copy(step, which).start()
    own = [pltpu.make_async_copy(src, dst, own_sem.at[i]) for i, (src, dst) in enumerate(wide_parts(x))]
    for copy in own:
        copy.start()

    for step in range(RING):
        for which in range(2):
            both_copy(step, which).wait_recv()

    def chunk_rows(t, rows):
        return pl.ds(pl.multiple_of(t * rows, rows), rows)

    def first_copy(t):
        src = both_g.at[:, chunk_rows(t, CROSS_ROWS)]
        return remote(src, slots.at[t], slot_send.at[t], slot_recv.at[t], across)

    def later_copy(t):
        return remote(staged.at[t], slots.at[t + AHEAD], slot_send.at[t + AHEAD], slot_recv.at[t + AHEAD], across)

    for t in range(AHEAD):
        first_copy(t).start()

    for copy in own:
        copy.wait()
    for which in (2, 0, 1):
        for step in range(1, RING):
            wide_copy(step, which).wait_recv()

    for i in range(2):
        sums_hid[i] = stats_g[0] + jnp.concatenate([marks[i]] * RING, axis=1)

    grads = functools.partial(
        chunk_grads, delta_ref=stats_g.at[1], query_ref=query_g, grad_ref=grad_g, acc_ref=acc
    )

    gives = jnp.broadcast_to(marks[1][0:1, :], (CROSS_ROWS, LANES)) > 0.5

    def slot_copy(t):
        return remote(slots.at[t], slots.at[t], slot_send.at[t], slot_recv.at[t], across)

    def out_copy(t):
        part = lax.rem(t, PER_DEVICE)
        rows = chunk_rows(part, CROSS_ROWS)
        cols = pl.ds(pl.multiple_of(x * LANES, LANES), LANES)
        return remote(
            both_s.at[t],
            both_out.at[:, rows, cols],
            out_send.at[t],
            out_recv.at[x, part],
            at_x("before", t // PER_DEVICE),
        )

    def finish(t):
        rows = chunk_rows(t, CROSS_ROWS)
        for which in range(2):
            came = jnp.where(gives, slots[t + AHEAD, which].astype(jnp.float32), 0.0)
            both_s[t, which] = (kept[which, rows] + came).astype(jnp.bfloat16)
        out_copy(t).start()

    def cross_step(t, carry):
        slot_copy(t).wait_recv()
        far = [jnp.where(gives, 0.0, slots[t, which].astype(jnp.float32)) for which in range(2)]
        out = grads(far[0], far[1], sums_hid.at[1])
        rows = chunk_rows(jnp.minimum(t + AHEAD, CROSS - 1), CROSS_ROWS)
        for which in range(2):
            given = both_g[which, rows].astype(jnp.float32)
            staged[t, which] = jnp.where(gives, given, out[which]).astype(jnp.bfloat16)
        later_copy(t).start()
        rows = chunk_rows(t, CROSS_ROWS)
        kept[0, rows], kept[1, rows] = grads(both_g[0, rows], both_g[1, rows], sums_hid.at[0])

        @pl.when(t >= AHEAD)
        def _():
            finish(t - AHEAD)

        return carry

    lax.fori_loop(0, CROSS, cross_step, 0)

    def back_copy(step):
        cols = pl.ds(pl.multiple_of(x * WIDTH, LANES), WIDTH)
        return remote(
            query_s.at[step],
            query_out.at[:, cols],
            back_send.at[step - 1],
            back_recv.at[step - 1],
            at_x("same", peer(step)),
        )

    for step in (1, 2, 3, 0):
        lanes = pl.ds(pl.multiple_of(peer(step) * TOK, LANES), TOK)
        turned = acc[:, lanes].T.astype(jnp.bfloat16)
        if step == 0:
            query_out[:, pl.ds(pl.multiple_of(x * WIDTH, LANES), WIDTH)] = turned
        else:
            query_s[step] = turned
            back_copy(step).start()

    def last_step(t, carry):
        slot_copy(t).wait_recv()
        finish(t - AHEAD)
        return carry

    lax.fori_loop(CROSS, SLOTS, last_step, 0)

    for step in range(1, RING):
        back_copy(step).wait_recv()

    def arrived(i, carry):
        where, part = i // PER_DEVICE, lax.rem(i, PER_DEVICE)
        cols = pl.ds(pl.multiple_of(where * LANES, LANES), LANES)
        dst = both_out.at[:, chunk_rows(part, CROSS_ROWS), cols]
        remote(both_s.at[0], dst, out_send.at[0], out_recv.at[where, part], across).wait_recv()
        return carry

    lax.fori_loop(0, RING * PER_DEVICE, arrived, 0)

    for step in range(RING):
        for which in range(2):
            both_copy(step, which).wait_send()
    for step in range(1, RING):
        for which in range(3):
            wide_copy(step, which).wait_send()
        back_copy(step).wait_send()
    for t in range(AHEAD):
        first_copy(t).wait_send()
    for t in range(CROSS):
        later_copy(t).wait_send()
        out_copy(t).wait_send()


def per_device(n_blk, queries, key_states, value_states, attn_out, grad_out, log_sums, owners):
    heads, wide = log_sums.shape[1], jnp.float32
    hbm, vmem = pl.BlockSpec(memory_space=pltpu.HBM), pl.BlockSpec(memory_space=pltpu.VMEM)
    smem = pl.BlockSpec(memory_space=pltpu.SMEM)
    narrow = jnp.bfloat16
    dma = pltpu.SemaphoreType.DMA
    grad_query, both = pl.pallas_call(
        functools.partial(kernel, n_blk),
        out_shape=(
            jax.ShapeDtypeStruct((TOK, heads * HEAD_DIM), narrow),
            jax.ShapeDtypeStruct((2, TOK, RING * LANES), narrow),
        ),
        in_specs=[hbm, hbm, hbm, hbm, hbm, hbm, smem],
        out_specs=(vmem, vmem),
        scratch_shapes=[
            pltpu.VMEM((TOK, heads * HEAD_DIM), narrow),
            pltpu.VMEM((TOK, heads * HEAD_DIM), narrow),
            pltpu.VMEM((2, heads, TOK), wide),
            pltpu.VMEM((HALF, WIDTH), narrow),
            pltpu.VMEM((HALF, WIDTH), narrow),
            pltpu.VMEM((2, HALF, LANES), narrow),
            pltpu.VMEM((2, HEADS_LOCAL, HALF), wide),
            pltpu.VMEM((2, HEADS_LOCAL, HALF), wide),
            pltpu.VMEM((WIDTH, HALF), wide),
            pltpu.VMEM((2, HALF, LANES), wide),
            pltpu.VMEM((SLOTS, 2, CROSS_ROWS, LANES), narrow),
            pltpu.VMEM((CROSS, 2, CROSS_ROWS, LANES), narrow),
            pltpu.VMEM((RING, TOK, WIDTH), narrow),
            pltpu.VMEM((CROSS, 2, CROSS_ROWS, LANES), narrow),
            dma((RING - 1, 3)),
            dma((RING - 1, 3)),
            dma((RING, 2)),
            dma((RING, 2)),
            dma((SLOTS,)),
            dma((SLOTS,)),
            dma((RING - 1,)),
            dma((RING - 1,)),
            dma((CROSS,)),
            dma((RING, PER_DEVICE)),
            dma((3,)),
            dma((3,)),
        ],
        compiler_params=pltpu.CompilerParams(
            collective_id=0, has_side_effects=True, vmem_limit_bytes=67043328
        ),
    )(queries, grad_out, key_states, value_states, attn_out, log_sums.T, owners)
    return (grad_query, both[0], both[1])


def solution(mesh):
    rows = P(("blk", "ulysses"), None)
    return jax.shard_map(
        functools.partial(per_device, mesh.shape["blk"]),
        mesh=mesh,
        in_specs=(rows, rows, rows, rows, rows, rows, P(None)),
        out_specs=(rows, rows, rows),
        check_vma=False,
    )
```

```python
import functools
import math

import jax
import jax.numpy as jnp
from jax import lax
from jax.experimental import pallas as pl
from jax.experimental.pallas import tpu as pltpu
from jax.sharding import PartitionSpec as P

HEAD_DIM = 64
LANES = 128
TOK = 128
RING = 4
HALF = TOK * RING
HEADS_LOCAL = 8
PAIRS = HEADS_LOCAL // 2
WIDTH = HEADS_LOCAL * HEAD_DIM
CROSS = 16
CROSS_ROWS = HALF // CROSS
AHEAD = 5
SLOTS = CROSS + AHEAD
NEAR_ROWS = 128
EARLY = 2
PER_DEVICE = TOK // CROSS_ROWS
TURN = 32
LEGS = 4
HIDE = 1e30
MESH = pl.DeviceIdType.MESH


def dot_nt(a, b):
    return lax.dot_general(a, b, (((1,), (1,)), ((), ())), preferred_element_type=jnp.float32)


def dot(a, b):
    return jnp.dot(a, b, preferred_element_type=jnp.float32)


def chunk_grads(key, value, sums_ref, delta_ref, query_ref, grad_ref, acc_ref):
    rows = key.shape[0]
    low = lax.broadcasted_iota(jnp.int32, (rows, LANES), 1) < HEAD_DIM
    zero = jnp.zeros((rows, LANES), jnp.float32)

    def spread(array, head):
        rolled = pltpu.roll(array, HEAD_DIM, 1)
        first, second = (array, rolled) if head == 0 else (rolled, array)
        return jnp.concatenate([jnp.where(low, first, zero), jnp.where(low, zero, second)], axis=0)

    def gather(first, second):
        one = first[:rows] + pltpu.roll(first[rows:], HEAD_DIM, 1)
        two = pltpu.roll(second[:rows], HEAD_DIM, 1) + second[rows:]
        return jnp.where(low, one, two)

    factor = 1.0 / math.sqrt(HEAD_DIM)
    key_f = key.astype(jnp.float32)
    value_f = value.astype(jnp.float32) * factor
    key_sums, value_sums = [], []
    for head in range(2):
        key_wide = spread(key_f, head)
        key_turned = key_wide.T.astype(jnp.bfloat16)
        key_wide = (key_wide * factor).astype(jnp.bfloat16)
        value_wide = spread(value_f, head).astype(jnp.bfloat16)
        key_sum, value_sum = None, None
        for pair in (2 * head, 2 * head + 1):
            cols = pl.ds(pair * LANES, LANES)
            query, grad = query_ref[:, cols], grad_ref[:, cols]
            scores = dot_nt(key_wide, query)
            dprobs = dot_nt(value_wide, grad)
            probs_b, dscores = [], []
            for one in range(2):
                part = slice(one * rows, (one + 1) * rows)
                at = pl.ds(2 * pair + one, 1)
                probs = jnp.exp(scores[part] - sums_ref[at, :])
                probs_b.append(probs.astype(jnp.bfloat16))
                dscores.append((probs * (dprobs[part] - delta_ref[at, :])).astype(jnp.bfloat16))
            probs_b = jnp.concatenate(probs_b, axis=0)
            dscores = jnp.concatenate(dscores, axis=0)
            value_piece, key_piece = dot(probs_b, grad), dot(dscores, query)
            value_sum = value_piece if value_sum is None else value_sum + value_piece
            key_sum = key_piece if key_sum is None else key_sum + key_piece
            acc_ref[cols, :] += dot(key_turned, dscores)
        key_sums.append(key_sum)
        value_sums.append(value_sum)
    return (gather(*key_sums), gather(*value_sums))


def kernel(
    n_blk,
    query_in,
    grad_in,
    key_in,
    value_in,
    out_in,
    sums_in,
    owners,
    query_out,
    both_out,
    grad_v,
    out_v,
    stats_in,
    query_g,
    grad_g,
    both_g,
    stats_g,
    sums_hid,
    acc,
    kept,
    slots,
    staged,
    query_s,
    both_s,
    wide_send,
    wide_recv,
    both_send,
    both_recv,
    slot_send,
    slot_recv,
    back_send,
    back_recv,
    out_send,
    out_recv,
    own_sem,
    load_sem,
    word_sem,
):
    blk, lane = lax.axis_index("blk"), lax.axis_index("ulysses")
    x, side = lax.rem(lane, RING), lane // RING
    after, before = lax.rem(blk + 1, n_blk), lax.rem(blk + n_blk - 1, n_blk)
    across = (blk, (1 - side) * RING + x)

    def turned(block):
        wraps = jnp.where(lax.rem(block, TURN) == 0, 1, 0)
        return lax.rem(side + wraps, 2)

    near = {"after": (after, turned(after)), "before": (before, turned(blk)), "same": (blk, side)}

    def along(steps):
        row = TURN // 2
        spot = lax.rem(side * row + lax.rem(blk, TURN) // 2 + steps + 2 * row, 2 * row)
        there = (blk // TURN) * TURN + lax.rem(spot, row) * 2 + lax.rem(blk, 2)
        return (there, (spot // row) * RING + x)

    leg = TURN // 2 // LEGS

    def peer(step):
        return lax.rem(x + step, RING)

    def at_x(name, where):
        block, half = near[name]
        return (block, half * RING + where)

    def remote(src, dst, send, recv, device):
        return pltpu.make_async_remote_copy(
            src_ref=src, dst_ref=dst, send_sem=send, recv_sem=recv, device_id=device, device_id_type=MESH
        )

    barrier = pltpu.get_barrier_semaphore()
    friends = [along(leg), along(-leg)] + [at_x("same", peer(step)) for step in range(1, RING)]
    friends += [at_x(name, peer(step)) for name in ("after", "before") for step in range(RING)]
    for friend in friends:
        pl.semaphore_signal(barrier, inc=1, device_id=friend, device_id_type=MESH)

    loads = [
        pltpu.make_async_copy(src, dst, load_sem.at[i])
        for i, (src, dst) in enumerate(((grad_in, grad_v), (out_in, out_v), (sums_in, stats_in.at[0])))
    ]
    for copy in loads:
        copy.start()
    pl.semaphore_wait(barrier, len(friends))

    def rows_of(where):
        return pl.ds(pl.multiple_of(where * TOK, TOK), TOK)

    mine = rows_of(x)

    def both_copy(step, which):
        to = peer(step)
        cols = pl.ds(pl.multiple_of(to * LANES, LANES), LANES)
        src = (key_in, value_in)[which].at[:, cols]
        return remote(
            src, both_g.at[which, mine], both_send.at[step, which], both_recv.at[step, which], at_x("after", to)
        )

    for step in range(RING):
        for which in range(2):
            both_copy(step, which).start()

    def wide_parts(to):
        cols = pl.ds(pl.multiple_of(to * WIDTH, LANES), WIDTH)
        heads = pl.ds(pl.multiple_of(to * HEADS_LOCAL, HEADS_LOCAL), HEADS_LOCAL)
        lanes = pl.ds(pl.multiple_of(x * TOK, LANES), TOK)
        return (
            (query_in.at[:, cols], query_g.at[mine]),
            (grad_in.at[:, cols], grad_g.at[mine]),
            (stats_in.at[:, heads], stats_g.at[:, :, lanes]),
        )

    def wide_copy(step, which):
        src, dst = wide_parts(peer(step))[which]
        return remote(
            src, dst, wide_send.at[step - 1, which], wide_recv.at[step - 1, which], at_x("same", peer(step))
        )

    for which in (0, 1):
        for step in range(1, RING):
            wide_copy(step, which).start()

    def pass_word(stop):
        pl.semaphore_signal(word_sem.at[stop], inc=1, device_id=along(-leg), device_id_type=MESH)

    pass_word(0)
    acc[...] = jnp.zeros_like(acc)
    query_half = jnp.full((HEADS_LOCAL, LANES), owners[2 * blk + side], jnp.int32)
    near_half = jnp.full((HEADS_LOCAL, LANES), owners[2 * before + near["before"][1]], jnp.int32)
    far_half = jnp.full((HEADS_LOCAL, LANES), owners[2 * before + 1 - near["before"][1]], jnp.int32)
    marks = [jnp.where(query_half > other, 0.0, HIDE) for other in (near_half, far_half)]
    for copy in loads:
        copy.wait()
    factor = 1.0 / math.sqrt(HEAD_DIM)
    for i in range(grad_v.shape[1] // LANES):
        cols = pl.ds(i * LANES, LANES)
        product = (grad_v[:, cols].astype(jnp.float32) * out_v[:, cols].astype(jnp.float32)).T
        for one in range(2):
            total = jnp.sum(product[one * HEAD_DIM : (one + 1) * HEAD_DIM], axis=0, keepdims=True)
            stats_in[1, pl.ds(2 * i + one, 1), :] = total * factor

    for stop in range(1, LEGS - 1):
        pl.semaphore_wait(word_sem.at[stop - 1], 1)
        pass_word(stop)
    for step in range(1, RING):
        wide_copy(step, 2).start()
    own = [pltpu.make_async_copy(src, dst, own_sem.at[i]) for i, (src, dst) in enumerate(wide_parts(x))]
    for copy in own:
        copy.start()

    for step in range(RING):
        for which in range(2):
            both_copy(step, which).wait_recv()
    pl.semaphore_wait(word_sem.at[LEGS - 2], 1)

    def chunk_rows(t, rows):
        return pl.ds(pl.multiple_of(t * rows, rows), rows)

    def first_copy(t):
        src = both_g.at[:, chunk_rows(t, CROSS_ROWS)]
        return remote(src, slots.at[t], slot_send.at[t], slot_recv.at[t], across)

    def later_copy(t):
        return remote(staged.at[t], slots.at[t + AHEAD], slot_send.at[t + AHEAD], slot_recv.at[t + AHEAD], across)

    for t in range(AHEAD):
        first_copy(t).start()

    for copy in own:
        copy.wait()
    for which in (2, 0, 1):
        for step in range(1, RING):
            wide_copy(step, which).wait_recv()

    for i in range(2):
        sums_hid[i] = stats_g[0] + jnp.concatenate([marks[i]] * RING, axis=1)

    grads = functools.partial(
        chunk_grads, delta_ref=stats_g.at[1], query_ref=query_g, grad_ref=grad_g, acc_ref=acc
    )

    def near_step(t, carry):
        rows = chunk_rows(t, NEAR_ROWS)
        kept[0, rows], kept[1, rows] = grads(both_g[0, rows], both_g[1, rows], sums_hid.at[0])
        return carry

    lax.fori_loop(0, EARLY, near_step, 0)
    ready = EARLY * NEAR_ROWS // CROSS_ROWS + AHEAD

    gives = jnp.broadcast_to(marks[1][0:1, :], (CROSS_ROWS, LANES)) > 0.5

    def slot_copy(t):
        return remote(slots.at[t], slots.at[t], slot_send.at[t], slot_recv.at[t], across)

    def out_copy(t):
        part = lax.rem(t, PER_DEVICE)
        rows = chunk_rows(part, CROSS_ROWS)
        cols = pl.ds(pl.multiple_of(x * LANES, LANES), LANES)
        return remote(
            both_s.at[t],
            both_out.at[:, rows, cols],
            out_send.at[t],
            out_recv.at[x, part],
            at_x("before", t // PER_DEVICE),
        )

    def finish(t):
        rows = chunk_rows(t, CROSS_ROWS)
        for which in range(2):
            came = jnp.where(gives, slots[t + AHEAD, which].astype(jnp.float32), 0.0)
            both_s[t, which] = (kept[which, rows] + came).astype(jnp.bfloat16)
        out_copy(t).start()

    def cross_step(t, carry):
        slot_copy(t).wait_recv()
        far = [jnp.where(gives, 0.0, slots[t, which].astype(jnp.float32)) for which in range(2)]
        out = grads(far[0], far[1], sums_hid.at[1])
        rows = chunk_rows(jnp.minimum(t + AHEAD, CROSS - 1), CROSS_ROWS)
        for which in range(2):
            given = both_g[which, rows].astype(jnp.float32)
            staged[t, which] = jnp.where(gives, given, out[which]).astype(jnp.bfloat16)
        later_copy(t).start()

        @pl.when((t >= AHEAD) & (t < ready))
        def _():
            finish(t - AHEAD)

        return carry

    lax.fori_loop(0, CROSS, cross_step, 0)
    lax.fori_loop(EARLY, HALF // NEAR_ROWS, near_step, 0)

    def back_copy(step):
        cols = pl.ds(pl.multiple_of(x * WIDTH, LANES), WIDTH)
        return remote(
            query_s.at[step],
            query_out.at[:, cols],
            back_send.at[step - 1],
            back_recv.at[step - 1],
            at_x("same", peer(step)),
        )

    for step in (1, 2, 3, 0):
        lanes = pl.ds(pl.multiple_of(peer(step) * TOK, LANES), TOK)
        turned = acc[:, lanes].T.astype(jnp.bfloat16)
        if step == 0:
            query_out[:, pl.ds(pl.multiple_of(x * WIDTH, LANES), WIDTH)] = turned
        else:
            query_s[step] = turned
            back_copy(step).start()

    def late_step(t, carry):
        finish(t - AHEAD)
        return carry

    def last_step(t, carry):
        slot_copy(t).wait_recv()
        finish(t - AHEAD)
        return carry

    lax.fori_loop(ready, CROSS, late_step, 0)
    lax.fori_loop(CROSS, SLOTS, last_step, 0)

    for step in range(1, RING):
        back_copy(step).wait_recv()

    def arrived(i, carry):
        where, part = i // PER_DEVICE, lax.rem(i, PER_DEVICE)
        cols = pl.ds(pl.multiple_of(where * LANES, LANES), LANES)
        dst = both_out.at[:, chunk_rows(part, CROSS_ROWS), cols]
        remote(both_s.at[0], dst, out_send.at[0], out_recv.at[where, part], across).wait_recv()
        return carry

    lax.fori_loop(0, RING * PER_DEVICE, arrived, 0)

    for step in range(RING):
        for which in range(2):
            both_copy(step, which).wait_send()
    for step in range(1, RING):
        for which in range(3):
            wide_copy(step, which).wait_send()
        back_copy(step).wait_send()
    for t in range(AHEAD):
        first_copy(t).wait_send()
    for t in range(CROSS):
        later_copy(t).wait_send()
        out_copy(t).wait_send()


def per_device(n_blk, queries, key_states, value_states, attn_out, grad_out, log_sums, owners):
    heads, wide = log_sums.shape[1], jnp.float32
    hbm, vmem = pl.BlockSpec(memory_space=pltpu.HBM), pl.BlockSpec(memory_space=pltpu.VMEM)
    smem = pl.BlockSpec(memory_space=pltpu.SMEM)
    narrow = jnp.bfloat16
    dma = pltpu.SemaphoreType.DMA
    grad_query, both = pl.pallas_call(
        functools.partial(kernel, n_blk),
        out_shape=(
            jax.ShapeDtypeStruct((TOK, heads * HEAD_DIM), narrow),
            jax.ShapeDtypeStruct((2, TOK, RING * LANES), narrow),
        ),
        in_specs=[hbm, hbm, hbm, hbm, hbm, hbm, smem],
        out_specs=(vmem, vmem),
        scratch_shapes=[
            pltpu.VMEM((TOK, heads * HEAD_DIM), narrow),
            pltpu.VMEM((TOK, heads * HEAD_DIM), narrow),
            pltpu.VMEM((2, heads, TOK), wide),
            pltpu.VMEM((HALF, WIDTH), narrow),
            pltpu.VMEM((HALF, WIDTH), narrow),
            pltpu.VMEM((2, HALF, LANES), narrow),
            pltpu.VMEM((2, HEADS_LOCAL, HALF), wide),
            pltpu.VMEM((2, HEADS_LOCAL, HALF), wide),
            pltpu.VMEM((WIDTH, HALF), wide),
            pltpu.VMEM((2, HALF, LANES), wide),
            pltpu.VMEM((SLOTS, 2, CROSS_ROWS, LANES), narrow),
            pltpu.VMEM((CROSS, 2, CROSS_ROWS, LANES), narrow),
            pltpu.VMEM((RING, TOK, WIDTH), narrow),
            pltpu.VMEM((CROSS, 2, CROSS_ROWS, LANES), narrow),
            dma((RING - 1, 3)),
            dma((RING - 1, 3)),
            dma((RING, 2)),
            dma((RING, 2)),
            dma((SLOTS,)),
            dma((SLOTS,)),
            dma((RING - 1,)),
            dma((RING - 1,)),
            dma((CROSS,)),
            dma((RING, PER_DEVICE)),
            dma((3,)),
            dma((3,)),
            pltpu.SemaphoreType.REGULAR((LEGS - 1,)),
        ],
        compiler_params=pltpu.CompilerParams(
            collective_id=0, has_side_effects=True, vmem_limit_bytes=67043328
        ),
    )(queries, grad_out, key_states, value_states, attn_out, log_sums.T, owners)
    return (grad_query, both[0], both[1])


def solution(mesh):
    rows = P(("blk", "ulysses"), None)
    return jax.shard_map(
        functools.partial(per_device, mesh.shape["blk"]),
        mesh=mesh,
        in_specs=(rows, rows, rows, rows, rows, rows, P(None)),
        out_specs=(rows, rows, rows),
        check_vma=False,
    )
```

```python
import functools
import math

import jax
import jax.numpy as jnp
from jax import lax
from jax.experimental import pallas as pl
from jax.experimental.pallas import tpu as pltpu
from jax.sharding import PartitionSpec as P

HEAD_DIM = 64
LANES = 128
TOK = 128
RING = 4
HALF = TOK * RING
HEADS_LOCAL = 8
PAIRS = HEADS_LOCAL // 2
WIDTH = HEADS_LOCAL * HEAD_DIM
CROSS = 16
CROSS_ROWS = HALF // CROSS
AHEAD = 5
SLOTS = CROSS + AHEAD
NEAR_ROWS = 128
EARLY = 2
PER_DEVICE = TOK // CROSS_ROWS
TURN = 32
LEGS = 4
HIDE = 1e30
MESH = pl.DeviceIdType.MESH


def dot_nt(a, b):
    return lax.dot_general(a, b, (((1,), (1,)), ((), ())), preferred_element_type=jnp.float32)


def dot(a, b):
    return jnp.dot(a, b, preferred_element_type=jnp.float32)


def chunk_grads(key, value, sums_ref, at_row, delta_ref, query_ref, grad_ref, keys_ref, dscores_ref):
    rows = key.shape[0]
    low = lax.broadcasted_iota(jnp.int32, (rows, LANES), 1) < HEAD_DIM
    zero = jnp.zeros((rows, LANES), jnp.float32)

    def spread(array, head):
        rolled = pltpu.roll(array, HEAD_DIM, 1)
        first, second = (array, rolled) if head == 0 else (rolled, array)
        return jnp.concatenate([jnp.where(low, first, zero), jnp.where(low, zero, second)], axis=0)

    def gather(first, second):
        one = first[:rows] + pltpu.roll(first[rows:], HEAD_DIM, 1)
        two = pltpu.roll(second[:rows], HEAD_DIM, 1) + second[rows:]
        return jnp.where(low, one, two)

    factor = 1.0 / math.sqrt(HEAD_DIM)
    key_f = key.astype(jnp.float32)
    value_f = value.astype(jnp.float32) * factor
    key_sums, value_sums = [], []
    for head in range(2):
        key_wide = spread(key_f, head)
        kept_rows = pl.ds(pl.multiple_of(at_row, 2 * rows), 2 * rows)
        keys_ref[head, kept_rows] = key_wide.astype(jnp.bfloat16)
        key_wide = (key_wide * factor).astype(jnp.bfloat16)
        value_wide = spread(value_f, head).astype(jnp.bfloat16)
        key_sum, value_sum = None, None
        for pair in (2 * head, 2 * head + 1):
            cols = pl.ds(pair * LANES, LANES)
            query, grad = query_ref[:, cols], grad_ref[:, cols]
            scores = dot_nt(key_wide, query)
            dprobs = dot_nt(value_wide, grad)
            probs_b, dscores = [], []
            for one in range(2):
                part = slice(one * rows, (one + 1) * rows)
                at = pl.ds(2 * pair + one, 1)
                probs = jnp.exp(scores[part] - sums_ref[at, :])
                probs_b.append(probs.astype(jnp.bfloat16))
                dscores.append((probs * (dprobs[part] - delta_ref[at, :])).astype(jnp.bfloat16))
            probs_b = jnp.concatenate(probs_b, axis=0)
            dscores = jnp.concatenate(dscores, axis=0)
            value_piece, key_piece = dot(probs_b, grad), dot(dscores, query)
            value_sum = value_piece if value_sum is None else value_sum + value_piece
            key_sum = key_piece if key_sum is None else key_sum + key_piece
            dscores_ref[pair, kept_rows] = dscores
        key_sums.append(key_sum)
        value_sums.append(value_sum)
    return (gather(*key_sums), gather(*value_sums))


def kernel(
    n_blk,
    query_in,
    grad_in,
    key_in,
    value_in,
    out_in,
    sums_in,
    owners,
    query_out,
    both_out,
    grad_v,
    out_v,
    stats_in,
    query_g,
    grad_g,
    both_g,
    stats_g,
    sums_hid,
    acc,
    keys_s,
    dscores_s,
    kept,
    slots,
    staged,
    query_s,
    both_s,
    wide_send,
    wide_recv,
    both_send,
    both_recv,
    slot_send,
    slot_recv,
    back_send,
    back_recv,
    out_send,
    out_recv,
    own_sem,
    load_sem,
    word_sem,
):
    blk, lane = lax.axis_index("blk"), lax.axis_index("ulysses")
    x, side = lax.rem(lane, RING), lane // RING
    after, before = lax.rem(blk + 1, n_blk), lax.rem(blk + n_blk - 1, n_blk)
    across = (blk, (1 - side) * RING + x)

    def turned(block):
        wraps = jnp.where(lax.rem(block, TURN) == 0, 1, 0)
        return lax.rem(side + wraps, 2)

    near = {"after": (after, turned(after)), "before": (before, turned(blk)), "same": (blk, side)}

    def along(steps):
        row = TURN // 2
        spot = lax.rem(side * row + lax.rem(blk, TURN) // 2 + steps + 2 * row, 2 * row)
        there = (blk // TURN) * TURN + lax.rem(spot, row) * 2 + lax.rem(blk, 2)
        return (there, (spot // row) * RING + x)

    leg = TURN // 2 // LEGS

    def peer(step):
        return lax.rem(x + step, RING)

    def at_x(name, where):
        block, half = near[name]
        return (block, half * RING + where)

    def remote(src, dst, send, recv, device):
        return pltpu.make_async_remote_copy(
            src_ref=src, dst_ref=dst, send_sem=send, recv_sem=recv, device_id=device, device_id_type=MESH
        )

    barrier = pltpu.get_barrier_semaphore()
    friends = [along(leg), along(-leg)] + [at_x("same", peer(step)) for step in range(1, RING)]
    friends += [at_x(name, peer(step)) for name in ("after", "before") for step in range(RING)]
    for friend in friends:
        pl.semaphore_signal(barrier, inc=1, device_id=friend, device_id_type=MESH)

    loads = [
        pltpu.make_async_copy(src, dst, load_sem.at[i])
        for i, (src, dst) in enumerate(((grad_in, grad_v), (out_in, out_v), (sums_in, stats_in.at[0])))
    ]
    for copy in loads:
        copy.start()
    pl.semaphore_wait(barrier, len(friends))

    def rows_of(where):
        return pl.ds(pl.multiple_of(where * TOK, TOK), TOK)

    mine = rows_of(x)

    def both_copy(step, which):
        to = peer(step)
        cols = pl.ds(pl.multiple_of(to * LANES, LANES), LANES)
        src = (key_in, value_in)[which].at[:, cols]
        return remote(
            src, both_g.at[which, mine], both_send.at[step, which], both_recv.at[step, which], at_x("after", to)
        )

    for step in range(RING):
        for which in range(2):
            both_copy(step, which).start()

    def wide_parts(to):
        cols = pl.ds(pl.multiple_of(to * WIDTH, LANES), WIDTH)
        heads = pl.ds(pl.multiple_of(to * HEADS_LOCAL, HEADS_LOCAL), HEADS_LOCAL)
        lanes = pl.ds(pl.multiple_of(x * TOK, LANES), TOK)
        return (
            (query_in.at[:, cols], query_g.at[mine]),
            (grad_in.at[:, cols], grad_g.at[mine]),
            (stats_in.at[:, heads], stats_g.at[:, :, lanes]),
        )

    def wide_copy(step, which):
        src, dst = wide_parts(peer(step))[which]
        return remote(
            src, dst, wide_send.at[step - 1, which], wide_recv.at[step - 1, which], at_x("same", peer(step))
        )

    for which in (0, 1):
        for step in range(1, RING):
            wide_copy(step, which).start()

    def pass_word(stop):
        pl.semaphore_signal(word_sem.at[stop], inc=1, device_id=along(-leg), device_id_type=MESH)

    pass_word(0)
    query_half = jnp.full((HEADS_LOCAL, LANES), owners[2 * blk + side], jnp.int32)
    near_half = jnp.full((HEADS_LOCAL, LANES), owners[2 * before + near["before"][1]], jnp.int32)
    far_half = jnp.full((HEADS_LOCAL, LANES), owners[2 * before + 1 - near["before"][1]], jnp.int32)
    marks = [jnp.where(query_half > other, 0.0, HIDE) for other in (near_half, far_half)]
    for copy in loads:
        copy.wait()
    factor = 1.0 / math.sqrt(HEAD_DIM)
    for i in range(grad_v.shape[1] // LANES):
        cols = pl.ds(i * LANES, LANES)
        product = (grad_v[:, cols].astype(jnp.float32) * out_v[:, cols].astype(jnp.float32)).T
        for one in range(2):
            total = jnp.sum(product[one * HEAD_DIM : (one + 1) * HEAD_DIM], axis=0, keepdims=True)
            stats_in[1, pl.ds(2 * i + one, 1), :] = total * factor

    for stop in range(1, LEGS - 1):
        pl.semaphore_wait(word_sem.at[stop - 1], 1)
        pass_word(stop)
    for step in range(1, RING):
        wide_copy(step, 2).start()
    own = [pltpu.make_async_copy(src, dst, own_sem.at[i]) for i, (src, dst) in enumerate(wide_parts(x))]
    for copy in own:
        copy.start()

    for step in range(RING):
        for which in range(2):
            both_copy(step, which).wait_recv()
    pl.semaphore_wait(word_sem.at[LEGS - 2], 1)

    def chunk_rows(t, rows):
        return pl.ds(pl.multiple_of(t * rows, rows), rows)

    def first_copy(t):
        src = both_g.at[:, chunk_rows(t, CROSS_ROWS)]
        return remote(src, slots.at[t], slot_send.at[t], slot_recv.at[t], across)

    def later_copy(t):
        return remote(staged.at[t], slots.at[t + AHEAD], slot_send.at[t + AHEAD], slot_recv.at[t + AHEAD], across)

    for t in range(AHEAD):
        first_copy(t).start()

    for copy in own:
        copy.wait()
    for which in (2, 0, 1):
        for step in range(1, RING):
            wide_copy(step, which).wait_recv()

    for i in range(2):
        sums_hid[i] = stats_g[0] + jnp.concatenate([marks[i]] * RING, axis=1)

    grads = functools.partial(
        chunk_grads, delta_ref=stats_g.at[1], query_ref=query_g, grad_ref=grad_g, keys_ref=keys_s, dscores_ref=dscores_s
    )

    def near_step(t, carry):
        rows = chunk_rows(t, NEAR_ROWS)
        kept[0, rows], kept[1, rows] = grads(both_g[0, rows], both_g[1, rows], sums_hid.at[0], t * (2 * NEAR_ROWS))
        return carry

    lax.fori_loop(0, EARLY, near_step, 0)
    ready = EARLY * NEAR_ROWS // CROSS_ROWS + AHEAD

    gives = jnp.broadcast_to(marks[1][0:1, :], (CROSS_ROWS, LANES)) > 0.5

    def slot_copy(t):
        return remote(slots.at[t], slots.at[t], slot_send.at[t], slot_recv.at[t], across)

    def out_copy(t):
        part = lax.rem(t, PER_DEVICE)
        rows = chunk_rows(part, CROSS_ROWS)
        cols = pl.ds(pl.multiple_of(x * LANES, LANES), LANES)
        return remote(
            both_s.at[t],
            both_out.at[:, rows, cols],
            out_send.at[t],
            out_recv.at[x, part],
            at_x("before", t // PER_DEVICE),
        )

    def finish(t):
        rows = chunk_rows(t, CROSS_ROWS)
        for which in range(2):
            came = jnp.where(gives, slots[t + AHEAD, which].astype(jnp.float32), 0.0)
            both_s[t, which] = (kept[which, rows] + came).astype(jnp.bfloat16)
        out_copy(t).start()

    def cross_step(t, carry):
        slot_copy(t).wait_recv()
        far = [jnp.where(gives, 0.0, slots[t, which].astype(jnp.float32)) for which in range(2)]
        out = grads(far[0], far[1], sums_hid.at[1], 2 * HALF + t * (2 * CROSS_ROWS))
        rows = chunk_rows(jnp.minimum(t + AHEAD, CROSS - 1), CROSS_ROWS)
        for which in range(2):
            given = both_g[which, rows].astype(jnp.float32)
            staged[t, which] = jnp.where(gives, given, out[which]).astype(jnp.bfloat16)
        later_copy(t).start()

        @pl.when((t >= AHEAD) & (t < ready))
        def _():
            finish(t - AHEAD)

        return carry

    lax.fori_loop(0, CROSS, cross_step, 0)
    lax.fori_loop(EARLY, HALF // NEAR_ROWS, near_step, 0)

    for head in range(2):
        keys_turned = keys_s[head].astype(jnp.float32).T.astype(jnp.bfloat16)
        for pair in (2 * head, 2 * head + 1):
            acc[pl.ds(pair * LANES, LANES), :] = dot(keys_turned, dscores_s[pair])

    def back_copy(step):
        cols = pl.ds(pl.multiple_of(x * WIDTH, LANES), WIDTH)
        return remote(
            query_s.at[step],
            query_out.at[:, cols],
            back_send.at[step - 1],
            back_recv.at[step - 1],
            at_x("same", peer(step)),
        )

    for step in (1, 2, 3, 0):
        lanes = pl.ds(pl.multiple_of(peer(step) * TOK, LANES), TOK)
        turned = acc[:, lanes].T.astype(jnp.bfloat16)
        if step == 0:
            query_out[:, pl.ds(pl.multiple_of(x * WIDTH, LANES), WIDTH)] = turned
        else:
            query_s[step] = turned
            back_copy(step).start()

    def late_step(t, carry):
        finish(t - AHEAD)
        return carry

    def last_step(t, carry):
        slot_copy(t).wait_recv()
        finish(t - AHEAD)
        return carry

    lax.fori_loop(ready, CROSS, late_step, 0)
    lax.fori_loop(CROSS, SLOTS, last_step, 0)

    for step in range(1, RING):
        back_copy(step).wait_recv()

    def arrived(i, carry):
        where, part = i // PER_DEVICE, lax.rem(i, PER_DEVICE)
        cols = pl.ds(pl.multiple_of(where * LANES, LANES), LANES)
        dst = both_out.at[:, chunk_rows(part, CROSS_ROWS), cols]
        remote(both_s.at[0], dst, out_send.at[0], out_recv.at[where, part], across).wait_recv()
        return carry

    lax.fori_loop(0, RING * PER_DEVICE, arrived, 0)

    for step in range(RING):
        for which in range(2):
            both_copy(step, which).wait_send()
    for step in range(1, RING):
        for which in range(3):
            wide_copy(step, which).wait_send()
        back_copy(step).wait_send()
    for t in range(AHEAD):
        first_copy(t).wait_send()
    for t in range(CROSS):
        later_copy(t).wait_send()
        out_copy(t).wait_send()


def per_device(n_blk, queries, key_states, value_states, attn_out, grad_out, log_sums, owners):
    heads, wide = log_sums.shape[1], jnp.float32
    hbm, vmem = pl.BlockSpec(memory_space=pltpu.HBM), pl.BlockSpec(memory_space=pltpu.VMEM)
    smem = pl.BlockSpec(memory_space=pltpu.SMEM)
    narrow = jnp.bfloat16
    dma = pltpu.SemaphoreType.DMA
    grad_query, both = pl.pallas_call(
        functools.partial(kernel, n_blk),
        out_shape=(
            jax.ShapeDtypeStruct((TOK, heads * HEAD_DIM), narrow),
            jax.ShapeDtypeStruct((2, TOK, RING * LANES), narrow),
        ),
        in_specs=[hbm, hbm, hbm, hbm, hbm, hbm, smem],
        out_specs=(vmem, vmem),
        scratch_shapes=[
            pltpu.VMEM((TOK, heads * HEAD_DIM), narrow),
            pltpu.VMEM((TOK, heads * HEAD_DIM), narrow),
            pltpu.VMEM((2, heads, TOK), wide),
            pltpu.VMEM((HALF, WIDTH), narrow),
            pltpu.VMEM((HALF, WIDTH), narrow),
            pltpu.VMEM((2, HALF, LANES), narrow),
            pltpu.VMEM((2, HEADS_LOCAL, HALF), wide),
            pltpu.VMEM((2, HEADS_LOCAL, HALF), wide),
            pltpu.VMEM((WIDTH, HALF), wide),
            pltpu.VMEM((2, 4 * HALF, LANES), narrow),
            pltpu.VMEM((PAIRS, 4 * HALF, HALF), narrow),
            pltpu.VMEM((2, HALF, LANES), wide),
            pltpu.VMEM((SLOTS, 2, CROSS_ROWS, LANES), narrow),
            pltpu.VMEM((CROSS, 2, CROSS_ROWS, LANES), narrow),
            pltpu.VMEM((RING, TOK, WIDTH), narrow),
            pltpu.VMEM((CROSS, 2, CROSS_ROWS, LANES), narrow),
            dma((RING - 1, 3)),
            dma((RING - 1, 3)),
            dma((RING, 2)),
            dma((RING, 2)),
            dma((SLOTS,)),
            dma((SLOTS,)),
            dma((RING - 1,)),
            dma((RING - 1,)),
            dma((CROSS,)),
            dma((RING, PER_DEVICE)),
            dma((3,)),
            dma((3,)),
            pltpu.SemaphoreType.REGULAR((LEGS - 1,)),
        ],
        compiler_params=pltpu.CompilerParams(
            collective_id=0, has_side_effects=True, vmem_limit_bytes=67043328
        ),
    )(queries, grad_out, key_states, value_states, attn_out, log_sums.T, owners)
    return (grad_query, both[0], both[1])


def solution(mesh):
    rows = P(("blk", "ulysses"), None)
    return jax.shard_map(
        functools.partial(per_device, mesh.shape["blk"]),
        mesh=mesh,
        in_specs=(rows, rows, rows, rows, rows, rows, P(None)),
        out_specs=(rows, rows, rows),
        check_vma=False,
    )
```

```python
import functools
import math

import jax
import jax.numpy as jnp
from jax import lax
from jax.experimental import pallas as pl
from jax.experimental.pallas import tpu as pltpu
from jax.sharding import PartitionSpec as P

HEAD_DIM = 64
LANES = 128
TOK = 128
RING = 4
HALF = TOK * RING
HEADS_LOCAL = 8
PAIRS = HEADS_LOCAL // 2
WIDTH = HEADS_LOCAL * HEAD_DIM
CROSS = 16
CROSS_ROWS = HALF // CROSS
AHEAD = 6
SLOTS = CROSS + AHEAD
NEAR_ROWS = 128
EARLY = 2
PER_DEVICE = TOK // CROSS_ROWS
TURN = 32
LEGS = 4
HIDE = 1e30
MESH = pl.DeviceIdType.MESH


def dot_nt(a, b):
    return lax.dot_general(a, b, (((1,), (1,)), ((), ())), preferred_element_type=jnp.float32)


def dot(a, b):
    return jnp.dot(a, b, preferred_element_type=jnp.float32)


def chunk_grads(key, value, sums_ref, at_row, delta_ref, query_ref, grad_ref, keys_ref, dscores_ref):
    rows = key.shape[0]
    low = lax.broadcasted_iota(jnp.int32, (rows, LANES), 1) < HEAD_DIM
    zero = jnp.zeros((rows, LANES), jnp.float32)

    def spread(array, head):
        rolled = pltpu.roll(array, HEAD_DIM, 1)
        first, second = (array, rolled) if head == 0 else (rolled, array)
        return jnp.concatenate([jnp.where(low, first, zero), jnp.where(low, zero, second)], axis=0)

    def gather(first, second):
        one = first[:rows] + pltpu.roll(first[rows:], HEAD_DIM, 1)
        two = pltpu.roll(second[:rows], HEAD_DIM, 1) + second[rows:]
        return jnp.where(low, one, two)

    factor = 1.0 / math.sqrt(HEAD_DIM)
    key_f = key.astype(jnp.float32)
    value_f = value.astype(jnp.float32) * factor
    key_sums, value_sums = [], []
    for head in range(2):
        key_wide = spread(key_f, head)
        kept_rows = pl.ds(pl.multiple_of(at_row, 2 * rows), 2 * rows)
        keys_ref[head, kept_rows] = key_wide.astype(jnp.bfloat16)
        key_wide = (key_wide * factor).astype(jnp.bfloat16)
        value_wide = spread(value_f, head).astype(jnp.bfloat16)
        key_sum, value_sum = None, None
        for pair in (2 * head, 2 * head + 1):
            cols = pl.ds(pair * LANES, LANES)
            query, grad = query_ref[:, cols], grad_ref[:, cols]
            scores = dot_nt(key_wide, query)
            dprobs = dot_nt(value_wide, grad)
            probs_b, dscores = [], []
            for one in range(2):
                part = slice(one * rows, (one + 1) * rows)
                at = pl.ds(2 * pair + one, 1)
                probs = jnp.exp(scores[part] - sums_ref[at, :])
                probs_b.append(probs.astype(jnp.bfloat16))
                dscores.append((probs * (dprobs[part] - delta_ref[at, :])).astype(jnp.bfloat16))
            probs_b = jnp.concatenate(probs_b, axis=0)
            dscores = jnp.concatenate(dscores, axis=0)
            value_piece, key_piece = dot(probs_b, grad), dot(dscores, query)
            value_sum = value_piece if value_sum is None else value_sum + value_piece
            key_sum = key_piece if key_sum is None else key_sum + key_piece
            dscores_ref[pair, kept_rows] = dscores
        key_sums.append(key_sum)
        value_sums.append(value_sum)
    return (gather(*key_sums), gather(*value_sums))


def kernel(
    n_blk,
    query_in,
    grad_in,
    key_in,
    value_in,
    out_in,
    sums_in,
    owners,
    query_out,
    both_out,
    grad_v,
    out_v,
    stats_in,
    query_g,
    grad_g,
    both_g,
    stats_g,
    sums_hid,
    acc,
    keys_s,
    dscores_s,
    kept,
    slots,
    staged,
    query_s,
    both_s,
    wide_send,
    wide_recv,
    both_send,
    both_recv,
    slot_send,
    slot_recv,
    back_send,
    back_recv,
    out_send,
    out_recv,
    own_sem,
    load_sem,
    word_sem,
):
    blk, lane = lax.axis_index("blk"), lax.axis_index("ulysses")
    x, side = lax.rem(lane, RING), lane // RING
    after, before = lax.rem(blk + 1, n_blk), lax.rem(blk + n_blk - 1, n_blk)
    across = (blk, (1 - side) * RING + x)

    def turned(block):
        wraps = jnp.where(lax.rem(block, TURN) == 0, 1, 0)
        return lax.rem(side + wraps, 2)

    near = {"after": (after, turned(after)), "before": (before, turned(blk)), "same": (blk, side)}

    def along(steps):
        row = TURN // 2
        spot = lax.rem(side * row + lax.rem(blk, TURN) // 2 + steps + 2 * row, 2 * row)
        there = (blk // TURN) * TURN + lax.rem(spot, row) * 2 + lax.rem(blk, 2)
        return (there, (spot // row) * RING + x)

    leg = TURN // 2 // LEGS

    def peer(step):
        return lax.rem(x + step, RING)

    def at_x(name, where):
        block, half = near[name]
        return (block, half * RING + where)

    def remote(src, dst, send, recv, device):
        return pltpu.make_async_remote_copy(
            src_ref=src, dst_ref=dst, send_sem=send, recv_sem=recv, device_id=device, device_id_type=MESH
        )

    barrier = pltpu.get_barrier_semaphore()
    friends = [along(leg), along(-leg)] + [at_x("same", peer(step)) for step in range(1, RING)]
    friends += [at_x(name, peer(step)) for name in ("after", "before") for step in range(RING)]
    for friend in friends:
        pl.semaphore_signal(barrier, inc=1, device_id=friend, device_id_type=MESH)

    loads = [
        pltpu.make_async_copy(src, dst, load_sem.at[i])
        for i, (src, dst) in enumerate(((grad_in, grad_v), (out_in, out_v), (sums_in, stats_in.at[0])))
    ]
    for copy in loads:
        copy.start()
    pl.semaphore_wait(barrier, len(friends))

    def rows_of(where):
        return pl.ds(pl.multiple_of(where * TOK, TOK), TOK)

    mine = rows_of(x)

    def both_copy(step, which):
        to = peer(step)
        cols = pl.ds(pl.multiple_of(to * LANES, LANES), LANES)
        src = (key_in, value_in)[which].at[:, cols]
        return remote(
            src, both_g.at[which, mine], both_send.at[step, which], both_recv.at[step, which], at_x("after", to)
        )

    for step in range(RING):
        for which in range(2):
            both_copy(step, which).start()

    def wide_parts(to):
        cols = pl.ds(pl.multiple_of(to * WIDTH, LANES), WIDTH)
        heads = pl.ds(pl.multiple_of(to * HEADS_LOCAL, HEADS_LOCAL), HEADS_LOCAL)
        lanes = pl.ds(pl.multiple_of(x * TOK, LANES), TOK)
        return (
            (query_in.at[:, cols], query_g.at[mine]),
            (grad_in.at[:, cols], grad_g.at[mine]),
            (stats_in.at[:, heads], stats_g.at[:, :, lanes]),
        )

    def wide_copy(step, which):
        src, dst = wide_parts(peer(step))[which]
        return remote(
            src, dst, wide_send.at[step - 1, which], wide_recv.at[step - 1, which], at_x("same", peer(step))
        )

    for which in (0, 1):
        for step in range(1, RING):
            wide_copy(step, which).start()

    def pass_word(stop):
        pl.semaphore_signal(word_sem.at[stop], inc=1, device_id=along(-leg), device_id_type=MESH)

    pass_word(0)
    query_half = jnp.full((HEADS_LOCAL, LANES), owners[2 * blk + side], jnp.int32)
    near_half = jnp.full((HEADS_LOCAL, LANES), owners[2 * before + near["before"][1]], jnp.int32)
    far_half = jnp.full((HEADS_LOCAL, LANES), owners[2 * before + 1 - near["before"][1]], jnp.int32)
    marks = [jnp.where(query_half > other, 0.0, HIDE) for other in (near_half, far_half)]
    for copy in loads:
        copy.wait()
    factor = 1.0 / math.sqrt(HEAD_DIM)
    for i in range(grad_v.shape[1] // LANES):
        cols = pl.ds(i * LANES, LANES)
        product = (grad_v[:, cols].astype(jnp.float32) * out_v[:, cols].astype(jnp.float32)).T
        for one in range(2):
            total = jnp.sum(product[one * HEAD_DIM : (one + 1) * HEAD_DIM], axis=0, keepdims=True)
            stats_in[1, pl.ds(2 * i + one, 1), :] = total * factor

    for stop in range(1, LEGS - 1):
        pl.semaphore_wait(word_sem.at[stop - 1], 1)
        pass_word(stop)
    for step in range(1, RING):
        wide_copy(step, 2).start()
    own = [pltpu.make_async_copy(src, dst, own_sem.at[i]) for i, (src, dst) in enumerate(wide_parts(x))]
    for copy in own:
        copy.start()

    for step in range(RING):
        for which in range(2):
            both_copy(step, which).wait_recv()
    pl.semaphore_wait(word_sem.at[LEGS - 2], 1)

    def chunk_rows(t, rows):
        return pl.ds(pl.multiple_of(t * rows, rows), rows)

    def first_copy(t):
        src = both_g.at[:, chunk_rows(t, CROSS_ROWS)]
        return remote(src, slots.at[t], slot_send.at[t], slot_recv.at[t], across)

    def later_copy(t):
        return remote(staged.at[t], slots.at[t + AHEAD], slot_send.at[t + AHEAD], slot_recv.at[t + AHEAD], across)

    for t in range(AHEAD):
        first_copy(t).start()

    for copy in own:
        copy.wait()
    for which in (2, 0, 1):
        for step in range(1, RING):
            wide_copy(step, which).wait_recv()

    for i in range(2):
        sums_hid[i] = stats_g[0] + jnp.concatenate([marks[i]] * RING, axis=1)

    grads = functools.partial(
        chunk_grads, delta_ref=stats_g.at[1], query_ref=query_g, grad_ref=grad_g, keys_ref=keys_s, dscores_ref=dscores_s
    )

    def near_step(t, carry):
        rows = chunk_rows(t, NEAR_ROWS)
        kept[0, rows], kept[1, rows] = grads(both_g[0, rows], both_g[1, rows], sums_hid.at[0], t * (2 * NEAR_ROWS))
        return carry

    lax.fori_loop(0, EARLY, near_step, 0)
    ready = EARLY * NEAR_ROWS // CROSS_ROWS + AHEAD

    gives = jnp.broadcast_to(marks[1][0:1, :], (CROSS_ROWS, LANES)) > 0.5

    def slot_copy(t):
        return remote(slots.at[t], slots.at[t], slot_send.at[t], slot_recv.at[t], across)

    def out_copy(t):
        part = lax.rem(t, PER_DEVICE)
        rows = chunk_rows(part, CROSS_ROWS)
        cols = pl.ds(pl.multiple_of(x * LANES, LANES), LANES)
        return remote(
            both_s.at[t],
            both_out.at[:, rows, cols],
            out_send.at[t],
            out_recv.at[x, part],
            at_x("before", t // PER_DEVICE),
        )

    def finish(t):
        rows = chunk_rows(t, CROSS_ROWS)
        for which in range(2):
            came = jnp.where(gives, slots[t + AHEAD, which].astype(jnp.float32), 0.0)
            both_s[t, which] = (kept[which, rows] + came).astype(jnp.bfloat16)
        out_copy(t).start()

    def cross_step(t, carry):
        slot_copy(t).wait_recv()
        far = [jnp.where(gives, 0.0, slots[t, which].astype(jnp.float32)) for which in range(2)]
        out = grads(far[0], far[1], sums_hid.at[1], 2 * HALF + t * (2 * CROSS_ROWS))
        rows = chunk_rows(jnp.minimum(t + AHEAD, CROSS - 1), CROSS_ROWS)
        for which in range(2):
            given = both_g[which, rows].astype(jnp.float32)
            staged[t, which] = jnp.where(gives, given, out[which]).astype(jnp.bfloat16)
        later_copy(t).start()

        @pl.when((t >= AHEAD) & (t < ready))
        def _():
            finish(t - AHEAD)

        return carry

    lax.fori_loop(0, CROSS, cross_step, 0)
    lax.fori_loop(EARLY, HALF // NEAR_ROWS, near_step, 0)

    for head in range(2):
        keys_turned = keys_s[head].astype(jnp.float32).T.astype(jnp.bfloat16)
        for pair in (2 * head, 2 * head + 1):
            acc[pl.ds(pair * LANES, LANES), :] = dot(keys_turned, dscores_s[pair])

    def back_copy(step):
        cols = pl.ds(pl.multiple_of(x * WIDTH, LANES), WIDTH)
        return remote(
            query_s.at[step],
            query_out.at[:, cols],
            back_send.at[step - 1],
            back_recv.at[step - 1],
            at_x("same", peer(step)),
        )

    for step in (1, 2, 3, 0):
        lanes = pl.ds(pl.multiple_of(peer(step) * TOK, LANES), TOK)
        turned = acc[:, lanes].T.astype(jnp.bfloat16)
        if step == 0:
            query_out[:, pl.ds(pl.multiple_of(x * WIDTH, LANES), WIDTH)] = turned
        else:
            query_s[step] = turned
            back_copy(step).start()

    def late_step(t, carry):
        finish(t - AHEAD)
        return carry

    def last_step(t, carry):
        slot_copy(t).wait_recv()
        finish(t - AHEAD)
        return carry

    lax.fori_loop(ready, CROSS, late_step, 0)
    lax.fori_loop(CROSS, SLOTS, last_step, 0)

    for step in range(1, RING):
        back_copy(step).wait_recv()

    def arrived(i, carry):
        where, part = i // PER_DEVICE, lax.rem(i, PER_DEVICE)
        cols = pl.ds(pl.multiple_of(where * LANES, LANES), LANES)
        dst = both_out.at[:, chunk_rows(part, CROSS_ROWS), cols]
        remote(both_s.at[0], dst, out_send.at[0], out_recv.at[where, part], across).wait_recv()
        return carry

    lax.fori_loop(0, RING * PER_DEVICE, arrived, 0)

    for step in range(RING):
        for which in range(2):
            both_copy(step, which).wait_send()
    for step in range(1, RING):
        for which in range(3):
            wide_copy(step, which).wait_send()
        back_copy(step).wait_send()
    for t in range(AHEAD):
        first_copy(t).wait_send()
    for t in range(CROSS):
        later_copy(t).wait_send()
        out_copy(t).wait_send()


def per_device(n_blk, queries, key_states, value_states, attn_out, grad_out, log_sums, owners):
    heads, wide = log_sums.shape[1], jnp.float32
    hbm, vmem = pl.BlockSpec(memory_space=pltpu.HBM), pl.BlockSpec(memory_space=pltpu.VMEM)
    smem = pl.BlockSpec(memory_space=pltpu.SMEM)
    narrow = jnp.bfloat16
    dma = pltpu.SemaphoreType.DMA
    grad_query, both = pl.pallas_call(
        functools.partial(kernel, n_blk),
        out_shape=(
            jax.ShapeDtypeStruct((TOK, heads * HEAD_DIM), narrow),
            jax.ShapeDtypeStruct((2, TOK, RING * LANES), narrow),
        ),
        in_specs=[hbm, hbm, hbm, hbm, hbm, hbm, smem],
        out_specs=(vmem, vmem),
        scratch_shapes=[
            pltpu.VMEM((TOK, heads * HEAD_DIM), narrow),
            pltpu.VMEM((TOK, heads * HEAD_DIM), narrow),
            pltpu.VMEM((2, heads, TOK), wide),
            pltpu.VMEM((HALF, WIDTH), narrow),
            pltpu.VMEM((HALF, WIDTH), narrow),
            pltpu.VMEM((2, HALF, LANES), narrow),
            pltpu.VMEM((2, HEADS_LOCAL, HALF), wide),
            pltpu.VMEM((2, HEADS_LOCAL, HALF), wide),
            pltpu.VMEM((WIDTH, HALF), wide),
            pltpu.VMEM((2, 4 * HALF, LANES), narrow),
            pltpu.VMEM((PAIRS, 4 * HALF, HALF), narrow),
            pltpu.VMEM((2, HALF, LANES), wide),
            pltpu.VMEM((SLOTS, 2, CROSS_ROWS, LANES), narrow),
            pltpu.VMEM((CROSS, 2, CROSS_ROWS, LANES), narrow),
            pltpu.VMEM((RING, TOK, WIDTH), narrow),
            pltpu.VMEM((CROSS, 2, CROSS_ROWS, LANES), narrow),
            dma((RING - 1, 3)),
            dma((RING - 1, 3)),
            dma((RING, 2)),
            dma((RING, 2)),
            dma((SLOTS,)),
            dma((SLOTS,)),
            dma((RING - 1,)),
            dma((RING - 1,)),
            dma((CROSS,)),
            dma((RING, PER_DEVICE)),
            dma((3,)),
            dma((3,)),
            pltpu.SemaphoreType.REGULAR((LEGS - 1,)),
        ],
        compiler_params=pltpu.CompilerParams(
            collective_id=0, has_side_effects=True, vmem_limit_bytes=67043328
        ),
    )(queries, grad_out, key_states, value_states, attn_out, log_sums.T, owners)
    return (grad_query, both[0], both[1])


def solution(mesh):
    rows = P(("blk", "ulysses"), None)
    return jax.shard_map(
        functools.partial(per_device, mesh.shape["blk"]),
        mesh=mesh,
        in_specs=(rows, rows, rows, rows, rows, rows, P(None)),
        out_specs=(rows, rows, rows),
        check_vma=False,
    )
```
